32 devices in a mesh: phase: 2 (over core), dp: 8 (over z, y), mp: 2 (over x).
Axes of the slice: x: 2, y: 2, z: 4, core: 2. Of those that a mesh axis runs over, the one named last changes fastest.
Arguments:
- segments: bfloat16 [2, 16, 64, 4096], P(None, 'dp', 'mp'), may hold values from -6 to 6
- memory_in: bfloat16 [16, 64, 4096], P('dp', 'mp'), may hold values from -6 to 6
- seg_lengths: int32 [2, 16], P(None, 'dp'), may hold values from 1 to 64, as said below
- routes: int32 [2, 8], replicated, may hold values from 0 to 7, each once within a row
- w_query: bfloat16 [2, 4096, 4096], P('phase', None, 'mp'), may hold values from -12 to 12
- w_key: bfloat16 [2, 4096, 1024], P('phase', None, 'mp'), may hold values from -1 to 1
- value_weight: bfloat16 [2, 4096, 1024], P('phase', None, 'mp'), may hold values from -0.09375 to 0.09375
- w_out: bfloat16 [2, 4096, 4096], P('phase', 'mp'), may hold values from -0.09375 to 0.09375
- norm_gain: bfloat16 [2, 4096], P('phase'), may hold values from 0.099609375 to 1.8984375
Outputs:
- mem_states: bfloat16 [2, 2, 16, 64, 4096], P('phase', None, 'dp', 'mp')
- seg_states: bfloat16 [2, 2, 16, 64, 4096], P('phase', None, 'dp', 'mp')
The draws below stay inside these ranges and needn't reach their ends.
Inputs may be any that keep to these rules, and one draw needn't show every extreme that they name: Each row m is a permutation of the data groups: slot m of group g hands its memory to slot m of group routes[m, g]. `seg_lengths`: some entry equals 64.
All inputs are finite; a program needn't handle non-finite values.
Results may differ from the reference program's by a relative error of at most 0.025.
Values may be sent and summed in bfloat16 or wider, within the bound.
No kernel may reach another device: no remote copies, remote signals or barrier semaphores. Data moves between devices by JAX's collectives and lax.ppermute only.
A program may use at most 192 MiB of HBM per device.

```python
from functools import partial
import jax
import jax.numpy as jnp
from jax import lax

MODEL_WIDTH = 4096
QUERY_HEADS = 32
KEY_VALUE_HEADS = 8
HEAD_SIZE = 128
MEM = 64
SEG = 64
ROUNDS = 2
MB = 2
SLOTS = 16
N_PHASE = 2
N_DP = 8
N_MP = 2


def paired_weights(key):
    leading_key, second_key = jax.random.split(jax.random.fold_in(key, 11), 2)
    fanin_scale = MODEL_WIDTH ** (-0.5)
    key_matrices = jnp.clip(jax.random.normal(leading_key, (N_PHASE, MODEL_WIDTH, KEY_VALUE_HEADS * HEAD_SIZE), jnp.float32), -6.0, 6.0) * fanin_scale
    drawn_query = jnp.clip(jax.random.normal(second_key, (N_PHASE, MODEL_WIDTH, QUERY_HEADS * HEAD_SIZE), jnp.float32), -6.0, 6.0) * fanin_scale
    return (key_matrices, drawn_query)


def draw_w_key(key, part):
    key_matrices, drawn_query = paired_weights(key)
    return key_matrices.astype(jnp.bfloat16)


def draw_w_query(key, part):
    key_matrices, drawn_query = paired_weights(key)
    return drawn_query.astype(jnp.bfloat16)


def draw_seg_lengths(key, part):
    leading_key, second_key = jax.random.split(jax.random.fold_in(key, 23), 2)
    lengths = jax.random.randint(leading_key, (ROUNDS * SLOTS,), 1, SEG + 1)
    full_spot = jax.random.randint(second_key, (), 0, ROUNDS * SLOTS)
    lengths = jnp.where(jnp.arange(ROUNDS * SLOTS) == full_spot, SEG, lengths)
    return lengths.reshape(ROUNDS, SLOTS).astype(jnp.int32)


def steps_of(stream_key, dims, pieces, smallest, top_value):
    factor_of, own = 1.0, jax.random.fold_in(stream_key, 6)
    for dim, parts in pieces:
        heights = jnp.exp(jax.random.uniform(jax.random.fold_in(own, dim), (parts,), jnp.float32, smallest / len(pieces), top_value / len(pieces)))
        factor_of = factor_of * jnp.repeat(heights, dims[dim] // parts).reshape([-1 if axis == dim else 1 for axis in range(len(dims))])
    return factor_of


def normal_values(stream_key, extent, spread, limit, pieces=(), held_as=jnp.bfloat16):
    array = spread * jax.random.normal(stream_key, extent, jnp.float32)
    if pieces:
        array = array * steps_of(stream_key, extent, pieces, -0.22, 0.18)
    return jnp.clip(array, -limit, limit).astype(held_as)


def setup_inputs(seed: int = 0) -> dict:
    arg_keys = jax.random.split(jax.random.key(seed), 10)
    segments = normal_values(arg_keys[0], (ROUNDS, SLOTS, SEG, MODEL_WIDTH), 1.0, 6.0, ((1, 8), (2, 2)))
    memory_in = normal_values(arg_keys[1], (SLOTS, MEM, MODEL_WIDTH), 1.0, 6.0, ((0, 8), (1, 2)))
    seg_lengths = draw_seg_lengths(jax.random.fold_in(arg_keys[9], 71), 0)
    routes = jax.vmap(lambda own: jax.random.permutation(own, N_DP))(jax.random.split(arg_keys[3], MB)).reshape((MB, N_DP)).astype(jnp.int32)
    w_query = draw_w_query(jax.random.fold_in(arg_keys[9], 71), 0)
    w_key = draw_w_key(jax.random.fold_in(arg_keys[9], 71), 0)
    value_weight = normal_values(arg_keys[6], (N_PHASE, MODEL_WIDTH, KEY_VALUE_HEADS * HEAD_SIZE), MODEL_WIDTH ** -0.5, 0.09375, ((0, 2), (2, 2)))
    w_out = normal_values(arg_keys[7], (N_PHASE, QUERY_HEADS * HEAD_SIZE, MODEL_WIDTH), (QUERY_HEADS * HEAD_SIZE) ** -0.5, 0.09375, ((0, 2), (1, 2)))
    norm_gain = jnp.clip(1.0 + 0.18 * jax.random.normal(arg_keys[8], (N_PHASE, MODEL_WIDTH), jnp.float32), 0.099609375, 1.8984375).astype(jnp.bfloat16)
    return dict(segments=segments, memory_in=memory_in, seg_lengths=seg_lengths, routes=routes, w_query=w_query, w_key=w_key, value_weight=value_weight, w_out=w_out, norm_gain=norm_gain)


EPSILON = 1e-05

def norm_rows(rows, gain):
    values = rows.astype(jnp.float32)
    scaled = values * lax.rsqrt(lax.optimization_barrier(jnp.mean(values * values, axis=-1, keepdims=True)) + EPSILON)
    return (scaled * gain.astype(jnp.float32)).astype(jnp.bfloat16)

def section_layer(mem_x, seg_x, length, w_query, w_key, value_weight, w_out, gain):
    combined = jnp.concatenate([mem_x, seg_x], axis=0)
    rows_total = combined.shape[0]
    normed = norm_rows(combined, gain)
    query_rows = jnp.dot(normed, w_query, preferred_element_type=jnp.float32).astype(jnp.bfloat16)
    rows_of_key = jnp.dot(normed, w_key, preferred_element_type=jnp.float32).astype(jnp.bfloat16)
    rows_of_value = jnp.dot(normed, value_weight, preferred_element_type=jnp.float32).astype(jnp.bfloat16)
    heads_of_query = query_rows.astype(jnp.float32).reshape(rows_total, KEY_VALUE_HEADS, QUERY_HEADS // KEY_VALUE_HEADS, HEAD_SIZE)
    heads_of_key = rows_of_key.astype(jnp.float32).reshape(rows_total, KEY_VALUE_HEADS, HEAD_SIZE)
    heads_of_value = rows_of_value.astype(jnp.float32).reshape(rows_total, KEY_VALUE_HEADS, HEAD_SIZE)
    scores = jnp.einsum('qcgd,kcd->cgqk', heads_of_query, heads_of_key) * HEAD_SIZE ** (-0.5)
    position = jnp.arange(rows_total, dtype=jnp.int32)
    query_pos = position[:, None]
    key_pos = position[None, :]
    visible = (key_pos < MEM) | (key_pos - MEM < length) & ((query_pos < MEM) | (key_pos <= query_pos))
    scores = jnp.where(visible, scores, -1e+30)
    row_max = lax.optimization_barrier(jnp.max(scores, axis=-1, keepdims=True))
    exponent = jnp.exp(scores - row_max)
    attn = (exponent / lax.optimization_barrier(jnp.sum(exponent, axis=-1, keepdims=True))).astype(jnp.bfloat16)
    attended = jnp.einsum('cgqk,kcd->qcgd', attn.astype(jnp.float32), heads_of_value)
    attended = attended.astype(jnp.bfloat16).reshape(rows_total, QUERY_HEADS * HEAD_SIZE)
    group_cols = QUERY_HEADS * HEAD_SIZE // N_MP
    head_sum = jnp.zeros((rows_total, MODEL_WIDTH), jnp.float32)
    for column_group in range(N_MP):
        lower = column_group * group_cols
        term = jnp.dot(attended[:, lower:lower + group_cols], w_out[lower:lower + group_cols], preferred_element_type=jnp.float32).astype(jnp.bfloat16)
        term = lax.optimization_barrier(term)
        head_sum = head_sum + term.astype(jnp.float32)
    layer_out = (combined.astype(jnp.float32) + head_sum).astype(jnp.bfloat16)
    return (layer_out[:MEM], layer_out[MEM:])

def run_section(packed, weights):
    return section_layer(packed[0], packed[1], packed[2], weights[0], weights[1], weights[2], weights[3], weights[4])

def reference(segments, memory_in, seg_lengths, routes, w_query, w_key, value_weight, w_out, norm_gain):
    memory = memory_in
    mem_record = [[] for section in range(N_PHASE)]
    seg_record = [[] for section in range(N_PHASE)]
    for round_index in range(ROUNDS):
        mem_rows = memory
        seg_rows = segments[round_index]
        for section in range(N_PHASE):
            weights = (w_query[section], w_key[section], value_weight[section], w_out[section], norm_gain[section])
            mem_rows, seg_rows = lax.map(partial(run_section, weights=weights), (mem_rows, seg_rows, seg_lengths[round_index]))
            mem_record[section].append(mem_rows)
            seg_record[section].append(seg_rows)
        if round_index + 1 < ROUNDS:
            source = mem_rows.reshape(N_DP, MB, MEM, MODEL_WIDTH).astype(jnp.float32)
            groups = jnp.arange(N_DP, dtype=jnp.int32)
            selector = (routes[:, None, :] == groups[None, :, None]).astype(jnp.float32)
            routed = jnp.einsum('mdg,gmre->dmre', selector, source, precision=lax.Precision.HIGHEST)
            memory = routed.reshape(N_DP * MB, MEM, MODEL_WIDTH).astype(jnp.bfloat16)
    mem_states = jnp.stack([jnp.stack(mem_record[section], 0) for section in range(N_PHASE)], 0)
    seg_states = jnp.stack([jnp.stack(seg_record[section], 0) for section in range(N_PHASE)], 0)
    return (mem_states, seg_states)
```

```python
import functools

import jax
import jax.numpy as jnp
from jax import lax
from jax.experimental import pallas as pl
from jax.experimental.pallas import tpu as pltpu
from jax.sharding import PartitionSpec as P


HEAD_SIZE = 128
EPSILON = 1e-05
TILE = 512
AXES = ("phase", "dp", "mp")
VMEM_SMALL = 16 << 20


ANY = pl.BlockSpec(memory_space=pl.ANY)
VMEM = pl.BlockSpec(memory_space=pltpu.VMEM)
SMEM = pl.BlockSpec(memory_space=pltpu.SMEM)
HBM = pl.BlockSpec(memory_space=pltpu.HBM)
BF16 = jnp.bfloat16
F32 = jnp.float32


def rows_of(count, width):
    return jax.ShapeDtypeStruct((count, width), BF16)


def column(j):
    return pl.ds(pl.multiple_of(j * TILE, TILE), TILE)


def out_tile(weights, first, q_dim, j):
    per_slab = weights.shape[1] // q_dim
    return weights.at[first + j // per_slab, pl.ds(pl.multiple_of(j % per_slab * q_dim, q_dim), q_dim)]


def load_kernel(w_query, w_key, value_weight, weights, sem):
    copies = []
    for source in (w_query, w_key, value_weight):
        for j in range(source.shape[1] // TILE):
            n = len(copies)
            copies.append(
                pltpu.make_async_copy(source.at[:, pl.ds(j * TILE, TILE)], weights.at[n], sem.at[n])
            )
    for copy in copies:
        copy.start()
    for copy in copies:
        copy.wait()


def load_weights(w_query, w_key, value_weight, w_out):
    width = w_query.shape[0]
    tiles = (w_query.shape[1] + w_key.shape[1] + value_weight.shape[1]) // TILE
    slabs = tiles + w_out.shape[0] * w_out.shape[1] // (width * TILE)
    return pl.pallas_call(
        load_kernel,
        out_shape=pltpu.VMEM((slabs, width, TILE), BF16),
        in_specs=[HBM] * 3,
        out_specs=VMEM,
        scratch_shapes=[pltpu.SemaphoreType.DMA((tiles,))],
        compiler_params=pltpu.CompilerParams(vmem_limit_bytes=VMEM_SMALL),
        cost_estimate=pl.CostEstimate(
            flops=0, bytes_accessed=2 * tiles * TILE * width, transcendentals=0
        ),
        name="load_weights",
    )(w_query, w_key, value_weight)


def section_kernel(cfg, plan, lengths, gain, *refs):
    round_index, slot, want, load, spots, q_tiles, k_tiles, half, ns = cfg
    refs = list(refs)
    blocks = [refs.pop(0) for _ in range(1 + max(s[0] for s in spots))]
    weights = refs.pop(0)
    w_out_in = refs.pop(0) if load else None
    if want:
        own_term, peer_term, x_own = [refs.pop(0) for _ in range(3)]
    else:
        term_out = refs.pop(0)
    if load:
        refs.pop(0)
    x, normed, qkv, attended = [refs.pop(0) for _ in range(4)]
    t_other = refs.pop(0) if want else None
    sem_in = refs.pop(0)
    sem_out = refs.pop(0) if load else None
    qkv_tiles, out_tiles = q_tiles + 2 * k_tiles, weights.shape[1] // TILE
    rows, q_dim = attended.shape
    nm = half - ns

    def in_copies():
        copies = []
        for n, (ref, index, first, to_other, at, size) in enumerate(spots):
            source = blocks[ref]
            if index:
                source = source.at[index]
            target = t_other if to_other else x
            copies.append(
                pltpu.make_async_copy(
                    source.at[pl.ds(first, size)], target.at[pl.ds(at, size)], sem_in.at[n]
                )
            )
        return copies

    def out_copy(j):
        return pltpu.make_async_copy(w_out_in.at[:, column(j)], out_tile(weights, qkv_tiles, q_dim, j), sem_out.at[j])

    active = plan[0] == want

    @pl.when(active)
    def _():
        for copy in in_copies():
            copy.start()

    if load:
        for j in range(out_tiles):
            out_copy(j).start()

    @pl.when(active)
    def _():
        for copy in in_copies():
            copy.wait()
        step = 16

        @pl.loop(0, rows // step)
        def _(b):
            at = pl.ds(pl.multiple_of(b * step, step), step)
            values = x[at, :].astype(F32)
            if want:
                rounded = (values + t_other[at, :].astype(F32)).astype(BF16)

                @pl.when(b * step < half)
                def _():
                    x_own[at, :] = rounded

                values = rounded.astype(F32)
            scale = lax.rsqrt(jnp.mean(values * values, axis=-1, keepdims=True) + EPSILON)
            normed[at, :] = (values * scale * gain[...].astype(F32)).astype(BF16)

        @pl.loop(0, qkv_tiles // 2)
        def _(pair):
            for u in range(2):
                j = pair * 2 + u
                qkv[j] = jnp.dot(normed[...], weights[j], preferred_element_type=F32).astype(BF16)

        mp = plan[1]
        length = lengths[round_index, slot]

        def place(axis):
            at = lax.broadcasted_iota(jnp.int32, (rows, rows), axis)
            inside = lax.rem(at, half)
            owner = jnp.where(at < half, mp, 1 - mp)
            return inside < nm, inside - nm + owner * ns

        query_mem, query_seg = place(0)
        key_mem, key_seg = place(1)
        visible = key_mem | (key_seg < length) & (query_mem | (key_seg <= query_seg))
        kv_heads = k_tiles * TILE // HEAD_SIZE
        per_group = (q_tiles * TILE // HEAD_SIZE) // kv_heads
        visible = jnp.concatenate([visible] * per_group, axis=0)

        def head(base, h):
            lane = (h * HEAD_SIZE) % TILE
            return qkv[base + h * HEAD_SIZE // TILE, :, lane : lane + HEAD_SIZE]

        for c in range(kv_heads):
            heads = [c * per_group + n for n in range(per_group)]
            queries = jnp.concatenate([head(0, h) for h in heads], axis=0)
            scores = lax.dot_general(
                queries, head(q_tiles, c), (((1,), (1,)), ((), ())), preferred_element_type=F32
            ) * HEAD_SIZE ** (-0.5)
            scores = jnp.where(visible, scores, -1e30)
            exponent = jnp.exp(scores - jnp.max(scores, axis=-1, keepdims=True))
            attn = (exponent / jnp.sum(exponent, axis=-1, keepdims=True)).astype(BF16)
            result = jnp.dot(attn, head(q_tiles + k_tiles, c), preferred_element_type=F32)
            for n, h in enumerate(heads):
                attended[:, h * HEAD_SIZE : (h + 1) * HEAD_SIZE] = result[
                    n * rows : (n + 1) * rows
                ].astype(BF16)

        @pl.loop(0, out_tiles // 2)
        def _(pair):
            for u in range(2):
                j = pair * 2 + u
                if load:
                    out_copy(j).wait()
                term = jnp.dot(
                    attended[...],
                    out_tile(weights, qkv_tiles, q_dim, j)[...],
                    preferred_element_type=F32,
                ).astype(BF16)
                if want:
                    own_term[:, column(j)] = term[:half]
                    peer_term[:, column(j)] = term[half:]
                else:
                    own = x[:half, column(j)].astype(F32) + term[:half].astype(F32)
                    term_out[:half, column(j)] = own.astype(BF16)
                    term_out[half:, column(j)] = term[half:]

    if load:

        @pl.when(jnp.logical_not(active))
        def _():
            for j in range(out_tiles):
                out_copy(j).wait()


def section(plan, lengths, gain, blocks, spots, weights, w_out, dims, round_index, slot, want):
    q_tiles, k_tiles, half, ns = dims
    load = w_out is not None
    width = weights.shape[1]
    rows, q_dim, qkv_tiles = 2 * half, q_tiles * TILE, q_tiles + 2 * k_tiles
    weights = pltpu.with_memory_space_constraint(weights, pltpu.VMEM)
    if want:
        out_shape = [rows_of(half, width)] * 3
    else:
        out_shape = [rows_of(rows, width)]
    aliases = {}
    if load:
        aliases[3 + len(blocks)] = len(out_shape)
        out_shape.append(pltpu.VMEM(weights.shape, BF16))
    scratch = [
        pltpu.VMEM((rows, width), BF16),
        pltpu.VMEM((rows, width), BF16),
        pltpu.VMEM((qkv_tiles, rows, TILE), BF16),
        pltpu.VMEM((rows, q_dim), BF16),
    ]
    if want:
        scratch.append(pltpu.VMEM((rows, width), BF16))
    scratch.append(pltpu.SemaphoreType.DMA((len(spots),)))
    if load:
        scratch.append(pltpu.SemaphoreType.DMA((width // TILE,)))
    return pl.pallas_call(
        functools.partial(
            section_kernel,
            (round_index, slot, want, load, tuple(spots), q_tiles, k_tiles, half, ns),
        ),
        out_shape=out_shape,
        in_specs=[SMEM, SMEM, VMEM] + [ANY] * len(blocks) + [VMEM] + [HBM] * load,
        out_specs=[VMEM] * len(out_shape),
        scratch_shapes=scratch,
        input_output_aliases=aliases,
        compiler_params=pltpu.CompilerParams(vmem_limit_bytes=VMEM_SMALL),
        cost_estimate=pl.CostEstimate(
            flops=2 * rows * width * (qkv_tiles * TILE + q_dim),
            bytes_accessed=2 * width * (qkv_tiles * TILE + q_dim),
            transcendentals=0,
        ),
    )(plan, lengths, gain, *blocks, weights, *([w_out] if load else []))


def pick_kernel(entries, count, plan, *refs):
    sources, targets, sem = refs[:count], refs[count:-1], refs[-1]

    @pl.when(plan[0] == 1)
    def _():
        for t, (target, entry) in enumerate(zip(targets, entries)):
            for n, source in enumerate(sources):

                @pl.when(plan[entry] == n)
                def _(source=source, target=target, t=t):
                    pltpu.make_async_copy(source, target, sem.at[t]).start()

        for t, target in enumerate(targets):
            pltpu.make_async_copy(sources[0], target, sem.at[t]).wait()


def pick(plan, entries, sources):
    shape = jax.ShapeDtypeStruct(sources[0].shape, sources[0].dtype)
    return pl.pallas_call(
        functools.partial(pick_kernel, tuple(entries), len(sources)),
        out_shape=[shape] * len(entries),
        in_specs=[SMEM] + [ANY] * len(sources),
        out_specs=[VMEM] * len(entries),
        scratch_shapes=[pltpu.SemaphoreType.DMA((len(entries),))],
        compiler_params=pltpu.CompilerParams(vmem_limit_bytes=4 << 20),
        name="pick",
    )(plan, *sources)


def finish_kernel(cfg, plan, x_own, own_term, arrived, back, *refs):
    round_index, slot, nm = cfg
    out_mem, out_seg, rows, term, other, sem = refs[-6:]
    half = rows.shape[0]

    def load(n, source, target):
        return pltpu.make_async_copy(source, target, sem.at[n])

    @pl.when(plan[0] == 0)
    def _():
        copy = load(0, back, rows)
        copy.start()
        copy.wait()

    @pl.when(plan[0] != 0)
    def _():
        copies = [load(0, x_own, rows), load(1, own_term, term), load(2, arrived, other)]
        for copy in copies:
            copy.start()
        for copy in copies:
            copy.wait()
        step = 16

        @pl.loop(0, half // step)
        def _(b):
            at = pl.ds(pl.multiple_of(b * step, step), step)
            added = term[at, :].astype(F32) + other[at, :].astype(F32)
            rows[at, :] = (rows[at, :].astype(F32) + added).astype(BF16)

    copies = [
        load(0, rows.at[pl.ds(0, nm)], out_mem.at[0, round_index, slot]),
        load(1, rows.at[pl.ds(nm, half - nm)], out_seg.at[0, round_index, slot]),
    ]
    for copy in copies:
        copy.start()
    for copy in copies:
        copy.wait()


def finish(plan, values, outs, shapes, round_index, slot, nm):
    half, width = values[0].shape
    return pl.pallas_call(
        functools.partial(finish_kernel, (round_index, slot, nm)),
        out_shape=[jax.ShapeDtypeStruct(shape, BF16) for shape in shapes],
        in_specs=[SMEM] + [ANY] * (4 + len(outs)),
        out_specs=[HBM] * 2,
        scratch_shapes=[pltpu.VMEM((half, width), BF16)] * 3 + [pltpu.SemaphoreType.DMA((3,))],
        input_output_aliases={5 + n: n for n in range(len(outs))},
        compiler_params=pltpu.CompilerParams(vmem_limit_bytes=4 << 20),
    )(plan, *values, *outs)


def per_device(
    segments, memory_in, seg_lengths, routes, w_query, w_key, value_weight, w_out, norm_gain
):
    rounds, slots = segments.shape[0], segments.shape[1]
    nm, ns = memory_in.shape[1], segments.shape[2]
    half = nm + ns
    groups = lax.axis_size("dp")
    phase, group, mp = (lax.axis_index(a) for a in AXES)
    inner = 2 if groups % 2 == 0 else 1
    outer = groups // inner

    def flat(p, g, i):
        return (p * groups + g) * 2 + i

    def send(value, pairs_of):
        pairs = [pair for g in range(groups) for i in range(2) for pair in pairs_of(g, i)]
        return lax.ppermute(value, AXES, pairs)

    def within(p):
        return lambda g, i: [(flat(p, g, i), flat(p, g, 1 - i))]

    def across(p, flip):
        return lambda g, i: [(flat(p, g, i), flat(1 - p, g, 1 - i if flip else i))]

    def along(step_outer, step_inner):
        def pairs(g, i):
            o, n = divmod(g, inner)
            target = (o + step_outer) % outer * inner + (n + step_inner) % inner
            return [(flat(1, g, i), flat(1, target, i))]

        return pairs

    ids = jnp.arange(groups, dtype=jnp.int32)
    mine_o, mine_n = group // inner, group % inner
    targets = mine_o * inner + (mine_n + jnp.arange(inner, dtype=jnp.int32)) % inner
    hit = routes[:, None, :] == targets[None, :, None]
    source = jnp.sum(jnp.where(hit, ids[None, None, :], 0), axis=-1)
    hops = (mine_o - source // inner + outer) % outer
    side = (mine_n - source[:, :1] % inner + inner) % inner
    entries = 1 + inner
    plan = jnp.concatenate(
        [
            jnp.stack([phase, mp]).astype(jnp.int32),
            jnp.concatenate([hops, side], axis=1).reshape(slots * entries),
        ]
    )

    def route(m, rows):
        base = 2 + m * entries
        held = [rows] + [send(rows, along(k, 0)) for k in range(1, outer)]
        picked = pick(plan, [base + k for k in range(inner)], held)
        if inner == 1:
            return picked[0]
        arrived = [send(picked[k], along(0, k)) for k in range(1, inner)]
        return pick(plan, [base + inner], [picked[0]] + arrived)[0]

    def gather_rows(m):
        rows = jnp.concatenate([memory_in[m], segments[0, m]], axis=0)
        return send(rows, within(0))

    weights = load_weights(w_query[0], w_key[0], value_weight[0], w_out[0])
    dims = (w_query.shape[2] // TILE, w_key.shape[2] // TILE, half, ns)
    first_peer = [gather_rows(m) for m in range(slots)]
    later_peer = send(segments[1:], within(0)) if rounds > 1 else None
    mem_own = mem_peer = None
    shapes = [(1, rounds, slots, n) + memory_in.shape[2:] for n in (nm, ns)]
    outs = []
    for r in range(rounds):
        sent = []
        for m in range(slots):
            if r == 0:
                blocks = [memory_in, segments, first_peer[m]]
                spots = [
                    (0, (m,), 0, False, 0, nm),
                    (1, (0, m), 0, False, nm, ns),
                    (2, (), 0, False, half, half),
                ]
            else:
                blocks = [mem_own[m], segments, mem_peer[m], later_peer]
                spots = [
                    (0, (), 0, False, 0, nm),
                    (1, (r, m), 0, False, nm, ns),
                    (2, (), 0, False, half, nm),
                    (3, (r - 1, m), 0, False, half + nm, ns),
                ]
            last = w_out[0] if r == 0 and m == 0 else None
            result = section(
                plan, seg_lengths, norm_gain, blocks, spots, weights, last, dims, r, m, 0
            )
            if len(result) == 2:
                weights = result[1]
            other = send(result[0], across(0, True))
            kept = send(result[0], across(0, False))
            sent.append((kept, other))
        spots = [
            (0, (), 0, False, 0, 2 * half),
            (1, (), half, True, 0, half),
            (1, (), 0, True, half, half),
        ]
        next_own, next_peer = [], []
        for m in range(slots):
            own_term, peer_term, x_own = section(
                plan, seg_lengths, norm_gain, sent[m], spots, weights, None, dims, r, m, 1
            )
            arrived = send(peer_term, within(1))
            back = send(x_own, across(1, False))
            if r + 1 < rounds:
                new_mem = (
                    x_own[:nm].astype(F32)
                    + (own_term[:nm].astype(F32) + arrived[:nm].astype(F32))
                ).astype(BF16)
                routed = route(m, new_mem)
                next_peer.append(send(routed, across(1, True)))
                next_own.append(send(routed, across(1, False)))
            outs = finish(plan, (x_own, own_term, arrived, back), outs, shapes, r, m, nm)
        mem_own, mem_peer = next_own, next_peer
    return tuple(outs)


def solution(mesh):
    specs = (
        P(None, "dp", "mp", None),
        P("dp", "mp", None),
        P(None, "dp"),
        P(),
        P("phase", None, "mp"),
        P("phase", None, "mp"),
        P("phase", None, "mp"),
        P("phase", "mp", None),
        P("phase", None),
    )
    out_specs = (P("phase", None, "dp", "mp", None), P("phase", None, "dp", "mp", None))
    step = jax.shard_map(
        per_device, mesh=mesh, in_specs=specs, out_specs=out_specs, check_vma=False
    )

    def run(segments, memory_in, *rest):
        whole = step
        return whole(segments, memory_in, *rest)

    return run
```

```python
import functools

import jax
import jax.numpy as jnp
from jax import lax
from jax.experimental import pallas as pl
from jax.experimental.pallas import tpu as pltpu
from jax.sharding import PartitionSpec as P


HEAD_SIZE = 128
EPSILON = 1e-05
TILE = 512
AXES = ("phase", "dp", "mp")
VMEM_SMALL = 14 << 20


ANY = pl.BlockSpec(memory_space=pl.ANY)
VMEM = pl.BlockSpec(memory_space=pltpu.VMEM)
SMEM = pl.BlockSpec(memory_space=pltpu.SMEM)
HBM = pl.BlockSpec(memory_space=pltpu.HBM)
BF16 = jnp.bfloat16
F32 = jnp.float32


def rows_of(count, width):
    return jax.ShapeDtypeStruct((count, width), BF16)


def column(j):
    return pl.ds(pl.multiple_of(j * TILE, TILE), TILE)


def out_tile(weights, first, q_dim, j):
    per_slab = weights.shape[1] // q_dim
    return weights.at[first + j // per_slab, pl.ds(pl.multiple_of(j % per_slab * q_dim, q_dim), q_dim)]


def load_kernel(plan, w_query, w_key, value_weight, weights, sem):
    copies = []
    for source in (w_query, w_key, value_weight):
        for j in range(source.shape[1] // TILE):
            n = len(copies)
            copies.append(
                pltpu.make_async_copy(source.at[:, pl.ds(j * TILE, TILE)], weights.at[n], sem.at[n])
            )
    for copy in copies:
        copy.start()
    for copy in copies:
        copy.wait()


def load_weights(plan, w_query, w_key, value_weight, w_out):
    width = w_query.shape[0]
    tiles = (w_query.shape[1] + w_key.shape[1] + value_weight.shape[1]) // TILE
    slabs = tiles + w_out.shape[0] * w_out.shape[1] // (width * TILE)
    return pl.pallas_call(
        load_kernel,
        out_shape=pltpu.VMEM((slabs, width, TILE), BF16),
        in_specs=[SMEM] + [HBM] * 3,
        out_specs=VMEM,
        scratch_shapes=[pltpu.SemaphoreType.DMA((tiles,))],
        compiler_params=pltpu.CompilerParams(vmem_limit_bytes=VMEM_SMALL),
        cost_estimate=pl.CostEstimate(
            flops=0, bytes_accessed=2 * tiles * TILE * width, transcendentals=0
        ),
        name="load_weights",
    )(plan, w_query, w_key, value_weight)


def section_kernel(cfg, plan, lengths, gain, *refs):
    round_index, slot, want, load, spots, q_tiles, k_tiles, half, ns = cfg
    refs = list(refs)
    blocks = [refs.pop(0) for _ in range(1 + max(s[0] for s in spots))]
    weights = refs.pop(0)
    w_out_in = refs.pop(0) if load else None
    if want:
        own_term, peer_term, x_own = [refs.pop(0) for _ in range(3)]
    else:
        term_out = refs.pop(0)
    if load:
        refs.pop(0)
    x, normed, qkv, attended = [refs.pop(0) for _ in range(4)]
    t_other = refs.pop(0) if want else None
    sem_in = refs.pop(0)
    sem_out = refs.pop(0) if load else None
    qkv_tiles, out_tiles = q_tiles + 2 * k_tiles, weights.shape[1] // TILE
    rows, q_dim = attended.shape
    nm = half - ns

    def in_copies():
        copies = []
        for n, (ref, index, first, to_other, at, size) in enumerate(spots):
            source = blocks[ref]
            if index:
                source = source.at[index]
            target = t_other if to_other else x
            copies.append(
                pltpu.make_async_copy(
                    source.at[pl.ds(first, size)], target.at[pl.ds(at, size)], sem_in.at[n]
                )
            )
        return copies

    def out_copy(j):
        return pltpu.make_async_copy(w_out_in.at[:, column(j)], out_tile(weights, qkv_tiles, q_dim, j), sem_out.at[j])

    active = plan[0] == want

    @pl.when(active)
    def _():
        for copy in in_copies():
            copy.start()

    def start_out():
        for j in range(out_tiles):
            out_copy(j).start()

    if load:
        pl.when(jnp.logical_not(active))(start_out)

    @pl.when(active)
    def _():
        for copy in in_copies():
            copy.wait()
        if load:
            start_out()
        step = 16

        @pl.loop(0, rows // step)
        def _(b):
            at = pl.ds(pl.multiple_of(b * step, step), step)
            values = x[at, :].astype(F32)
            if want:
                rounded = (values + t_other[at, :].astype(F32)).astype(BF16)

                @pl.when(b * step < half)
                def _():
                    x_own[at, :] = rounded

                values = rounded.astype(F32)
            scale = lax.rsqrt(jnp.mean(values * values, axis=-1, keepdims=True) + EPSILON)
            normed[at, :] = (values * scale * gain[...].astype(F32)).astype(BF16)

        @pl.loop(0, qkv_tiles // 2)
        def _(pair):
            for u in range(2):
                j = pair * 2 + u
                qkv[j] = jnp.dot(normed[...], weights[j], preferred_element_type=F32).astype(BF16)

        mp = plan[1]
        length = lengths[round_index, slot]

        def place(axis):
            at = lax.broadcasted_iota(jnp.int32, (rows, rows), axis)
            inside = lax.rem(at, half)
            owner = jnp.where(at < half, mp, 1 - mp)
            return inside < nm, inside - nm + owner * ns

        query_mem, query_seg = place(0)
        key_mem, key_seg = place(1)
        visible = key_mem | (key_seg < length) & (query_mem | (key_seg <= query_seg))
        kv_heads = k_tiles * TILE // HEAD_SIZE
        per_group = (q_tiles * TILE // HEAD_SIZE) // kv_heads
        visible = jnp.concatenate([visible] * per_group, axis=0)

        def head(base, h):
            lane = (h * HEAD_SIZE) % TILE
            return qkv[base + h * HEAD_SIZE // TILE, :, lane : lane + HEAD_SIZE]

        for c in range(kv_heads):
            heads = [c * per_group + n for n in range(per_group)]
            queries = jnp.concatenate([head(0, h) for h in heads], axis=0)
            scores = lax.dot_general(
                queries, head(q_tiles, c), (((1,), (1,)), ((), ())), preferred_element_type=F32
            ) * HEAD_SIZE ** (-0.5)
            scores = jnp.where(visible, scores, -1e30)
            exponent = jnp.exp(scores - jnp.max(scores, axis=-1, keepdims=True))
            attn = (exponent / jnp.sum(exponent, axis=-1, keepdims=True)).astype(BF16)
            result = jnp.dot(attn, head(q_tiles + k_tiles, c), preferred_element_type=F32)
            for n, h in enumerate(heads):
                attended[:, h * HEAD_SIZE : (h + 1) * HEAD_SIZE] = result[
                    n * rows : (n + 1) * rows
                ].astype(BF16)

        @pl.loop(0, out_tiles // 2)
        def _(pair):
            for u in range(2):
                j = pair * 2 + u
                if load:
                    out_copy(j).wait()
                term = jnp.dot(
                    attended[...],
                    out_tile(weights, qkv_tiles, q_dim, j)[...],
                    preferred_element_type=F32,
                ).astype(BF16)
                if want:
                    own_term[:, column(j)] = term[:half]
                    peer_term[:, column(j)] = term[half:]
                else:
                    own = x[:half, column(j)].astype(F32) + term[:half].astype(F32)
                    term_out[:half, column(j)] = own.astype(BF16)
                    term_out[half:, column(j)] = term[half:]

    if load:

        @pl.when(jnp.logical_not(active))
        def _():
            for j in range(out_tiles):
                out_copy(j).wait()


def section(plan, lengths, gain, blocks, spots, weights, w_out, dims, round_index, slot, want):
    q_tiles, k_tiles, half, ns = dims
    load = w_out is not None
    width = weights.shape[1]
    rows, q_dim, qkv_tiles = 2 * half, q_tiles * TILE, q_tiles + 2 * k_tiles
    weights = pltpu.with_memory_space_constraint(weights, pltpu.VMEM)
    near_blocks = (0, 1) if want else (2, 3) if round_index == 0 else (0, 2)
    blocks = [
        pltpu.with_memory_space_constraint(b, pltpu.VMEM) if n in near_blocks else b
        for n, b in enumerate(blocks)
    ]
    if want:
        out_shape = [rows_of(half, width)] * 3
    else:
        out_shape = [rows_of(rows, width)]
    aliases = {}
    if load:
        aliases[3 + len(blocks)] = len(out_shape)
        out_shape.append(pltpu.VMEM(weights.shape, BF16))
    scratch = [
        pltpu.VMEM((rows, width), BF16),
        pltpu.VMEM((rows, width), BF16),
        pltpu.VMEM((qkv_tiles, rows, TILE), BF16),
        pltpu.VMEM((rows, q_dim), BF16),
    ]
    if want:
        scratch.append(pltpu.VMEM((rows, width), BF16))
    scratch.append(pltpu.SemaphoreType.DMA((len(spots),)))
    if load:
        scratch.append(pltpu.SemaphoreType.DMA((width // TILE,)))
    return pl.pallas_call(
        functools.partial(
            section_kernel,
            (round_index, slot, want, load, tuple(spots), q_tiles, k_tiles, half, ns),
        ),
        out_shape=out_shape,
        in_specs=[SMEM, SMEM, VMEM] + [ANY] * len(blocks) + [VMEM] + [HBM] * load,
        out_specs=[VMEM] * len(out_shape),
        scratch_shapes=scratch,
        input_output_aliases=aliases,
        compiler_params=pltpu.CompilerParams(vmem_limit_bytes=VMEM_SMALL),
        cost_estimate=pl.CostEstimate(
            flops=2 * rows * width * (qkv_tiles * TILE + q_dim),
            bytes_accessed=2 * width * (qkv_tiles * TILE + q_dim),
            transcendentals=0,
        ),
    )(plan, lengths, gain, *blocks, weights, *([w_out] if load else []))


def pick_kernel(entries, count, plan, *refs):
    sources, targets, sem = refs[:count], refs[count:-1], refs[-1]

    @pl.when(plan[0] == 1)
    def _():
        for t, (target, entry) in enumerate(zip(targets, entries)):
            for n, source in enumerate(sources):

                @pl.when(plan[entry] == n)
                def _(source=source, target=target, t=t):
                    pltpu.make_async_copy(source, target, sem.at[t]).start()

        for t, target in enumerate(targets):
            pltpu.make_async_copy(sources[0], target, sem.at[t]).wait()


def pick(plan, entries, sources):
    shape = jax.ShapeDtypeStruct(sources[0].shape, sources[0].dtype)
    return pl.pallas_call(
        functools.partial(pick_kernel, tuple(entries), len(sources)),
        out_shape=[shape] * len(entries),
        in_specs=[SMEM] + [ANY] * len(sources),
        out_specs=[VMEM] * len(entries),
        scratch_shapes=[pltpu.SemaphoreType.DMA((len(entries),))],
        compiler_params=pltpu.CompilerParams(vmem_limit_bytes=4 << 20),
        name="pick",
    )(plan, *sources)


def finish_kernel(cfg, plan, x_own, own_term, arrived, back, *refs):
    round_index, slot, nm = cfg
    out_mem, out_seg, rows, term, other, sem = refs[-6:]
    half = rows.shape[0]

    def load(n, source, target):
        return pltpu.make_async_copy(source, target, sem.at[n])

    @pl.when(plan[0] == 0)
    def _():
        copy = load(0, back, rows)
        copy.start()
        copy.wait()

    @pl.when(plan[0] != 0)
    def _():
        copies = [load(0, x_own, rows), load(1, own_term, term), load(2, arrived, other)]
        for copy in copies:
            copy.start()
        for copy in copies:
            copy.wait()
        step = 16

        @pl.loop(0, half // step)
        def _(b):
            at = pl.ds(pl.multiple_of(b * step, step), step)
            added = term[at, :].astype(F32) + other[at, :].astype(F32)
            rows[at, :] = (rows[at, :].astype(F32) + added).astype(BF16)

    copies = [
        load(0, rows.at[pl.ds(0, nm)], out_mem.at[0, round_index, slot]),
        load(1, rows.at[pl.ds(nm, half - nm)], out_seg.at[0, round_index, slot]),
    ]
    for copy in copies:
        copy.start()
    for copy in copies:
        copy.wait()


def finish(plan, values, outs, shapes, round_index, slot, nm):
    half, width = values[0].shape
    return pl.pallas_call(
        functools.partial(finish_kernel, (round_index, slot, nm)),
        out_shape=[jax.ShapeDtypeStruct(shape, BF16) for shape in shapes],
        in_specs=[SMEM] + [ANY] * (4 + len(outs)),
        out_specs=[HBM] * 2,
        scratch_shapes=[pltpu.VMEM((half, width), BF16)] * 3 + [pltpu.SemaphoreType.DMA((3,))],
        input_output_aliases={5 + n: n for n in range(len(outs))},
        compiler_params=pltpu.CompilerParams(vmem_limit_bytes=4 << 20),
    )(plan, *values, *outs)


def per_device(
    segments, memory_in, seg_lengths, routes, w_query, w_key, value_weight, w_out, norm_gain
):
    rounds, slots = segments.shape[0], segments.shape[1]
    nm, ns = memory_in.shape[1], segments.shape[2]
    half = nm + ns
    groups = lax.axis_size("dp")
    phase, group, mp = (lax.axis_index(a) for a in AXES)
    inner = 2 if groups % 2 == 0 else 1
    outer = groups // inner

    def flat(p, g, i):
        return (p * groups + g) * 2 + i

    def send(value, pairs_of):
        pairs = [pair for g in range(groups) for i in range(2) for pair in pairs_of(g, i)]
        return lax.ppermute(value, AXES, pairs)

    def within(p):
        return lambda g, i: [(flat(p, g, i), flat(p, g, 1 - i))]

    def across(p, flip):
        return lambda g, i: [(flat(p, g, i), flat(1 - p, g, 1 - i if flip else i))]

    def hop(place, step):
        return place ^ step if outer & (outer - 1) == 0 else (place + step) % outer

    def along(step_outer, step_inner):
        def pairs(g, i):
            o, n = divmod(g, inner)
            target = hop(o, step_outer) * inner + (n + step_inner) % inner
            return [(flat(1, g, i), flat(1, target, i))]

        return pairs

    ids = jnp.arange(groups, dtype=jnp.int32)
    mine_o, mine_n = group // inner, group % inner
    targets = mine_o * inner + (mine_n + jnp.arange(inner, dtype=jnp.int32)) % inner
    hit = routes[:, None, :] == targets[None, :, None]
    source = jnp.sum(jnp.where(hit, ids[None, None, :], 0), axis=-1)
    source_o = source // inner
    if outer & (outer - 1) == 0:
        hops = (mine_o ^ source_o) & (outer - 1)
    else:
        hops = (mine_o - source_o + outer) % outer
    side = (mine_n - source[:, :1] % inner + inner) % inner
    entries = 1 + inner
    plan = jnp.concatenate(
        [
            jnp.stack([phase, mp]).astype(jnp.int32),
            jnp.concatenate([hops, side], axis=1).reshape(slots * entries),
        ]
    )

    def route(m, rows):
        base = 2 + m * entries
        held = [rows] + [send(rows, along(k, 0)) for k in range(1, outer)]
        picked = pick(plan, [base + k for k in range(inner)], held)
        if inner == 1:
            return picked[0]
        arrived = [send(picked[k], along(0, k)) for k in range(1, inner)]
        return pick(plan, [base + inner], [picked[0]] + arrived)[0]

    weights = load_weights(plan, w_query[0], w_key[0], value_weight[0], w_out[0])
    dims = (w_query.shape[2] // TILE, w_key.shape[2] // TILE, half, ns)
    first_mem = send(memory_in, within(0))
    first_seg = send(segments[:1], within(0))
    later_peer = None
    if rounds > 1:
        later_peer = send(segments[1:], within(1))
        later_peer = send(later_peer, across(1, False))
    mem_own = mem_peer = None
    shapes = [(1, rounds, slots, n) + memory_in.shape[2:] for n in (nm, ns)]
    outs = []
    for r in range(rounds):
        sent = []
        for m in range(slots):
            if r == 0:
                blocks = [memory_in, segments, first_mem, first_seg]
                spots = [
                    (0, (m,), 0, False, 0, nm),
                    (1, (0, m), 0, False, nm, ns),
                    (2, (m,), 0, False, half, nm),
                    (3, (0, m), 0, False, half + nm, ns),
                ]
            else:
                blocks = [mem_own[m], segments, mem_peer[m], later_peer]
                spots = [
                    (0, (), 0, False, 0, nm),
                    (1, (r, m), 0, False, nm, ns),
                    (2, (), 0, False, half, nm),
                    (3, (r - 1, m), 0, False, half + nm, ns),
                ]
            last = w_out[0] if r == 0 and m == 0 else None
            result = section(
                plan, seg_lengths, norm_gain, blocks, spots, weights, last, dims, r, m, 0
            )
            if len(result) == 2:
                weights = result[1]
            other = send(result[0], across(0, True))
            kept = send(result[0], across(0, False))
            sent.append((kept, other))
        spots = [
            (0, (), 0, False, 0, 2 * half),
            (1, (), half, True, 0, half),
            (1, (), 0, True, half, half),
        ]
        next_own, next_peer = [], []
        for m in range(slots):
            own_term, peer_term, x_own = section(
                plan, seg_lengths, norm_gain, sent[m], spots, weights, None, dims, r, m, 1
            )
            arrived = send(peer_term, within(1))
            back = send(x_own, across(1, False))
            if r + 1 < rounds:
                new_mem = (
                    x_own[:nm].astype(F32)
                    + (own_term[:nm].astype(F32) + arrived[:nm].astype(F32))
                ).astype(BF16)
                routed = route(m, new_mem)
                next_peer.append(send(routed, across(1, True)))
                next_own.append(send(routed, across(1, False)))
            values = (x_own, own_term, arrived, back)
            if r + 1 == rounds:
                values = [pltpu.with_memory_space_constraint(v, pltpu.VMEM) for v in values]
            outs = finish(plan, values, outs, shapes, r, m, nm)
        mem_own, mem_peer = next_own, next_peer
    return tuple(outs)


def solution(mesh):
    specs = (
        P(None, "dp", "mp", None),
        P("dp", "mp", None),
        P(None, "dp"),
        P(),
        P("phase", None, "mp"),
        P("phase", None, "mp"),
        P("phase", None, "mp"),
        P("phase", "mp", None),
        P("phase", None),
    )
    out_specs = (P("phase", None, "dp", "mp", None), P("phase", None, "dp", "mp", None))
    step = jax.shard_map(
        per_device, mesh=mesh, in_specs=specs, out_specs=out_specs, check_vma=False
    )

    def run(segments, memory_in, *rest):
        whole = step
        return whole(segments, memory_in, *rest)

    return run
```

```python
import functools

import jax
import jax.numpy as jnp
from jax import lax
from jax.experimental import pallas as pl
from jax.experimental.pallas import tpu as pltpu
from jax.sharding import PartitionSpec as P


HEAD_SIZE = 128
EPSILON = 1e-05
TILE = 512
AXES = ("phase", "dp", "mp")
VMEM_SMALL = 14 << 20


ANY = pl.BlockSpec(memory_space=pl.ANY)
VMEM = pl.BlockSpec(memory_space=pltpu.VMEM)
SMEM = pl.BlockSpec(memory_space=pltpu.SMEM)
HBM = pl.BlockSpec(memory_space=pltpu.HBM)
BF16 = jnp.bfloat16
F32 = jnp.float32


def column(j):
    return pl.ds(pl.multiple_of(j * TILE, TILE), TILE)


def out_tile(weights, first, q_dim, j):
    per_slab = weights.shape[1] // q_dim
    return weights.at[first + j // per_slab, pl.ds(pl.multiple_of(j % per_slab * q_dim, q_dim), q_dim)]


def load_kernel(plan, w_query, weights, sem):
    copies = [
        pltpu.make_async_copy(w_query.at[:, pl.ds(n * TILE, TILE)], weights.at[n], sem.at[n])
        for n in range(w_query.shape[1] // TILE)
    ]
    for copy in copies:
        copy.start()
    for copy in copies:
        copy.wait()


def load_weights(plan, w_query, w_key, value_weight, w_out):
    width = w_query.shape[0]
    loaded = w_query.shape[1] // TILE
    tiles = (w_query.shape[1] + w_key.shape[1] + value_weight.shape[1]) // TILE
    slabs = tiles + w_out.shape[0] * w_out.shape[1] // (width * TILE)
    return pl.pallas_call(
        load_kernel,
        out_shape=pltpu.VMEM((slabs, width, TILE), BF16),
        in_specs=[SMEM, HBM],
        out_specs=VMEM,
        scratch_shapes=[pltpu.SemaphoreType.DMA((loaded,))],
        compiler_params=pltpu.CompilerParams(vmem_limit_bytes=VMEM_SMALL),
        cost_estimate=pl.CostEstimate(
            flops=0, bytes_accessed=2 * loaded * TILE * width, transcendentals=0
        ),
        name="load_weights",
    )(plan, w_query)


def section_kernel(cfg, plan, lengths, gain, *refs):
    round_index, slot, want, load, spots, q_tiles, k_tiles, half, ns = cfg
    refs = list(refs)
    blocks = [refs.pop(0) for _ in range(1 + max(s[0] for s in spots))]
    weights = refs.pop(0)
    w_key, value_weight, w_out_in = [refs.pop(0) for _ in range(3)] if load else [None] * 3
    if want:
        own_term, peer_term, x_own = [refs.pop(0) for _ in range(3)]
    else:
        term_out = refs.pop(0)
    if load:
        refs.pop(0)
    x, normed, qkv, attended = [refs.pop(0) for _ in range(4)]
    t_other = refs.pop(0) if want else None
    sem_in = refs.pop(0)
    sem_kv, sem_out = [refs.pop(0) for _ in range(2)] if load else [None] * 2
    qkv_tiles, out_tiles = q_tiles + 2 * k_tiles, weights.shape[1] // TILE
    rows, q_dim = attended.shape
    nm = half - ns

    def in_copies():
        copies = []
        for n, (ref, index, first, to_other, at, size) in enumerate(spots):
            source = blocks[ref]
            if index:
                source = source.at[index]
            target = t_other if to_other else x
            copies.append(
                pltpu.make_async_copy(
                    source.at[pl.ds(first, size)], target.at[pl.ds(at, size)], sem_in.at[n]
                )
            )
        return copies

    def out_copy(j):
        return pltpu.make_async_copy(w_out_in.at[:, column(j)], out_tile(weights, qkv_tiles, q_dim, j), sem_out.at[j])

    def kv_copies():
        return [
            pltpu.make_async_copy(
                source.at[:, pl.ds(j * TILE, TILE)],
                weights.at[q_tiles + n * k_tiles + j],
                sem_kv.at[n * k_tiles + j],
            )
            for n, source in enumerate((w_key, value_weight))
            for j in range(k_tiles)
        ]

    active = plan[0] == want
    ahead = min(4, out_tiles)

    @pl.when(active)
    def _():
        for copy in in_copies():
            copy.start()

    if load:

        @pl.when(jnp.logical_not(active))
        def _():
            copies = kv_copies() + [out_copy(j) for j in range(out_tiles)]
            for copy in copies:
                copy.start()
            for copy in copies:
                copy.wait()

    @pl.when(active)
    def _():
        for copy in in_copies():
            copy.wait()
        if load:
            for copy in kv_copies():
                copy.start()
        step = 16

        @pl.loop(0, rows // step)
        def _(b):
            at = pl.ds(pl.multiple_of(b * step, step), step)
            values = x[at, :].astype(F32)
            if want:
                rounded = (values + t_other[at, :].astype(F32)).astype(BF16)

                @pl.when(b * step < half)
                def _():
                    x_own[at, :] = rounded

                values = rounded.astype(F32)
            scale = lax.rsqrt(jnp.mean(values * values, axis=-1, keepdims=True) + EPSILON)
            normed[at, :] = (values * scale * gain[...].astype(F32)).astype(BF16)

        def project(j):
            qkv[j] = jnp.dot(normed[...], weights[j], preferred_element_type=F32).astype(BF16)

        def project_pairs(first, last):
            @pl.loop(first, last)
            def _(pair):
                for u in range(2):
                    project(pair * 2 + u)

        if load:
            project_pairs(0, 1)
            for j in range(ahead):
                out_copy(j).start()
            project_pairs(1, q_tiles // 2)
            for copy in kv_copies():
                copy.wait()
            project_pairs(q_tiles // 2, qkv_tiles // 2)
        else:
            project_pairs(0, qkv_tiles // 2)

        mp = plan[1]
        length = lengths[round_index, slot]

        def place(axis):
            at = lax.broadcasted_iota(jnp.int32, (rows, rows), axis)
            inside = lax.rem(at, half)
            owner = jnp.where(at < half, mp, 1 - mp)
            return inside < nm, inside - nm + owner * ns

        query_mem, query_seg = place(0)
        key_mem, key_seg = place(1)
        visible = key_mem | (key_seg < length) & (query_mem | (key_seg <= query_seg))
        kv_heads = k_tiles * TILE // HEAD_SIZE
        per_group = (q_tiles * TILE // HEAD_SIZE) // kv_heads
        visible = jnp.concatenate([visible] * per_group, axis=0)

        def head(base, h):
            lane = (h * HEAD_SIZE) % TILE
            return qkv[base + h * HEAD_SIZE // TILE, :, lane : lane + HEAD_SIZE]

        for c in range(kv_heads):
            heads = [c * per_group + n for n in range(per_group)]
            queries = jnp.concatenate([head(0, h) for h in heads], axis=0)
            scores = lax.dot_general(
                queries, head(q_tiles, c), (((1,), (1,)), ((), ())), preferred_element_type=F32
            ) * HEAD_SIZE ** (-0.5)
            scores = jnp.where(visible, scores, -1e30)
            exponent = jnp.exp(scores - jnp.max(scores, axis=-1, keepdims=True))
            attn = (exponent / jnp.sum(exponent, axis=-1, keepdims=True)).astype(BF16)
            result = jnp.dot(attn, head(q_tiles + k_tiles, c), preferred_element_type=F32)
            for n, h in enumerate(heads):
                attended[:, h * HEAD_SIZE : (h + 1) * HEAD_SIZE] = result[
                    n * rows : (n + 1) * rows
                ].astype(BF16)

        @pl.loop(0, out_tiles // 2)
        def _(pair):
            for u in range(2):
                j = pair * 2 + u
                if load:
                    out_copy(j).wait()

                    @pl.when(j + ahead < out_tiles)
                    def _(j=j):
                        out_copy(j + ahead).start()

                term = jnp.dot(
                    attended[...],
                    out_tile(weights, qkv_tiles, q_dim, j)[...],
                    preferred_element_type=F32,
                ).astype(BF16)
                if want:
                    own_term[:, column(j)] = term[:half]
                    peer_term[:, column(j)] = term[half:]
                else:
                    own = x[:half, column(j)].astype(F32) + term[:half].astype(F32)
                    term_out[:half, column(j)] = own.astype(BF16)
                    term_out[half:, column(j)] = term[half:]


def section(plan, lengths, gain, blocks, spots, weights, w_out, dims, round_index, slot, want):
    q_tiles, k_tiles, half, ns = dims
    load = bool(w_out)
    width = weights.shape[1]
    rows, q_dim, qkv_tiles = 2 * half, q_tiles * TILE, q_tiles + 2 * k_tiles
    weights = pltpu.with_memory_space_constraint(weights, pltpu.VMEM)
    near_blocks = (0, 1) if want else (2, 3) if round_index == 0 else (0, 2)
    blocks = [
        pltpu.with_memory_space_constraint(b, pltpu.VMEM) if n in near_blocks else b
        for n, b in enumerate(blocks)
    ]
    if want:
        out_shape = [pltpu.VMEM((half, width), BF16)] * 3
    else:
        out_shape = [pltpu.VMEM((rows, width), BF16)]
    aliases = {}
    if load:
        aliases[3 + len(blocks)] = len(out_shape)
        out_shape.append(pltpu.VMEM(weights.shape, BF16))
    scratch = [
        pltpu.VMEM((rows, width), BF16),
        pltpu.VMEM((rows, width), BF16),
        pltpu.VMEM((qkv_tiles, rows, TILE), BF16),
        pltpu.VMEM((rows, q_dim), BF16),
    ]
    if want:
        scratch.append(pltpu.VMEM((rows, width), BF16))
    scratch.append(pltpu.SemaphoreType.DMA((len(spots),)))
    if load:
        scratch.append(pltpu.SemaphoreType.DMA((2 * k_tiles,)))
        scratch.append(pltpu.SemaphoreType.DMA((width // TILE,)))
    return pl.pallas_call(
        functools.partial(
            section_kernel,
            (round_index, slot, want, load, tuple(spots), q_tiles, k_tiles, half, ns),
        ),
        out_shape=out_shape,
        in_specs=[SMEM, SMEM, VMEM] + [ANY] * len(blocks) + [VMEM] + [HBM] * len(w_out),
        out_specs=[VMEM] * len(out_shape),
        scratch_shapes=scratch,
        input_output_aliases=aliases,
        compiler_params=pltpu.CompilerParams(vmem_limit_bytes=VMEM_SMALL),
        cost_estimate=pl.CostEstimate(
            flops=2 * rows * width * (qkv_tiles * TILE + q_dim),
            bytes_accessed=2 * width * (qkv_tiles * TILE + q_dim),
            transcendentals=0,
        ),
    )(plan, lengths, gain, *blocks, weights, *w_out)


def pick_kernel(entries, count, plan, *refs):
    sources, targets, sem = refs[:count], refs[count:-1], refs[-1]

    @pl.when(plan[0] == 1)
    def _():
        for t, (target, entry) in enumerate(zip(targets, entries)):
            for n, source in enumerate(sources):

                @pl.when(plan[entry] == n)
                def _(source=source, target=target, t=t):
                    pltpu.make_async_copy(source, target, sem.at[t]).start()

        for t, target in enumerate(targets):
            pltpu.make_async_copy(sources[0], target, sem.at[t]).wait()


def pick(plan, entries, sources):
    shape = jax.ShapeDtypeStruct(sources[0].shape, sources[0].dtype)
    return pl.pallas_call(
        functools.partial(pick_kernel, tuple(entries), len(sources)),
        out_shape=[shape] * len(entries),
        in_specs=[SMEM] + [ANY] * len(sources),
        out_specs=[VMEM] * len(entries),
        scratch_shapes=[pltpu.SemaphoreType.DMA((len(entries),))],
        compiler_params=pltpu.CompilerParams(vmem_limit_bytes=4 << 20),
        name="pick",
    )(plan, *sources)


def finish_kernel(cfg, plan, x_own, own_term, arrived, back, *refs):
    round_index, slot, nm = cfg
    out_mem, out_seg, rows, term, other, sem = refs[-6:]
    half = rows.shape[0]

    def load(n, source, target):
        return pltpu.make_async_copy(source, target, sem.at[n])

    @pl.when(plan[0] == 0)
    def _():
        copy = load(0, back, rows)
        copy.start()
        copy.wait()

    @pl.when(plan[0] != 0)
    def _():
        copies = [load(0, x_own, rows), load(1, own_term, term), load(2, arrived, other)]
        for copy in copies:
            copy.start()
        for copy in copies:
            copy.wait()
        step = 16

        @pl.loop(0, half // step)
        def _(b):
            at = pl.ds(pl.multiple_of(b * step, step), step)
            added = term[at, :].astype(F32) + other[at, :].astype(F32)
            rows[at, :] = (rows[at, :].astype(F32) + added).astype(BF16)

    copies = [
        load(0, rows.at[pl.ds(0, nm)], out_mem.at[0, round_index, slot]),
        load(1, rows.at[pl.ds(nm, half - nm)], out_seg.at[0, round_index, slot]),
    ]
    for copy in copies:
        copy.start()
    for copy in copies:
        copy.wait()


def finish(plan, values, outs, shapes, round_index, slot, nm):
    half, width = values[0].shape
    return pl.pallas_call(
        functools.partial(finish_kernel, (round_index, slot, nm)),
        out_shape=[jax.ShapeDtypeStruct(shape, BF16) for shape in shapes],
        in_specs=[SMEM] + [ANY] * (4 + len(outs)),
        out_specs=[HBM] * 2,
        scratch_shapes=[pltpu.VMEM((half, width), BF16)] * 3 + [pltpu.SemaphoreType.DMA((3,))],
        input_output_aliases={5 + n: n for n in range(len(outs))},
        compiler_params=pltpu.CompilerParams(vmem_limit_bytes=4 << 20),
    )(plan, *values, *outs)


def per_device(
    segments, memory_in, seg_lengths, routes, w_query, w_key, value_weight, w_out, norm_gain
):
    rounds, slots = segments.shape[0], segments.shape[1]
    nm, ns = memory_in.shape[1], segments.shape[2]
    half = nm + ns
    groups = lax.axis_size("dp")
    phase, group, mp = (lax.axis_index(a) for a in AXES)
    inner = 2 if groups % 2 == 0 else 1
    outer = groups // inner

    def flat(p, g, i):
        return (p * groups + g) * 2 + i

    def send(value, pairs_of):
        pairs = [pair for g in range(groups) for i in range(2) for pair in pairs_of(g, i)]
        return lax.ppermute(value, AXES, pairs)

    def within(p):
        return lambda g, i: [(flat(p, g, i), flat(p, g, 1 - i))]

    def across(p, flip):
        return lambda g, i: [(flat(p, g, i), flat(1 - p, g, 1 - i if flip else i))]

    def hop(place, step):
        return place ^ step if outer & (outer - 1) == 0 else (place + step) % outer

    def along(step_outer, step_inner):
        def pairs(g, i):
            o, n = divmod(g, inner)
            target = hop(o, step_outer) * inner + (n + step_inner) % inner
            return [(flat(1, g, i), flat(1, target, i))]

        return pairs

    ids = jnp.arange(groups, dtype=jnp.int32)
    mine_o, mine_n = group // inner, group % inner
    targets = mine_o * inner + (mine_n + jnp.arange(inner, dtype=jnp.int32)) % inner
    hit = routes[:, None, :] == targets[None, :, None]
    source = jnp.sum(jnp.where(hit, ids[None, None, :], 0), axis=-1)
    source_o = source // inner
    if outer & (outer - 1) == 0:
        hops = (mine_o ^ source_o) & (outer - 1)
    else:
        hops = (mine_o - source_o + outer) % outer
    side = (mine_n - source[:, :1] % inner + inner) % inner
    entries = 1 + inner
    plan = jnp.concatenate(
        [
            jnp.stack([phase, mp]).astype(jnp.int32),
            jnp.concatenate([hops, side], axis=1).reshape(slots * entries),
        ]
    )

    def route(m, rows):
        base = 2 + m * entries
        held = [rows] + [send(rows, along(k, 0)) for k in range(1, outer)]
        picked = pick(plan, [base + k for k in range(inner)], held)
        if inner == 1:
            return picked[0]
        arrived = [send(picked[k], along(0, k)) for k in range(1, inner)]
        return pick(plan, [base + inner], [picked[0]] + arrived)[0]

    weights = load_weights(plan, w_query[0], w_key[0], value_weight[0], w_out[0])
    dims = (w_query.shape[2] // TILE, w_key.shape[2] // TILE, half, ns)
    first_mem = send(memory_in, within(0))
    first_seg = send(segments[:1], within(0))
    later_peer = None
    if rounds > 1:
        later_peer = send(segments[1:], within(1))
        later_peer = send(later_peer, across(1, False))
    mem_own = mem_peer = None
    shapes = [(1, rounds, slots, n) + memory_in.shape[2:] for n in (nm, ns)]
    outs = []
    for r in range(rounds):
        sent = []
        for m in range(slots):
            if r == 0:
                blocks = [memory_in, segments, first_mem, first_seg]
                spots = [
                    (0, (m,), 0, False, 0, nm),
                    (1, (0, m), 0, False, nm, ns),
                    (2, (m,), 0, False, half, nm),
                    (3, (0, m), 0, False, half + nm, ns),
                ]
            else:
                blocks = [mem_own[m], segments, mem_peer[m], later_peer]
                spots = [
                    (0, (), 0, False, 0, nm),
                    (1, (r, m), 0, False, nm, ns),
                    (2, (), 0, False, half, nm),
                    (3, (r - 1, m), 0, False, half + nm, ns),
                ]
            last = (w_key[0], value_weight[0], w_out[0]) if r == 0 and m == 0 else ()
            result = section(
                plan, seg_lengths, norm_gain, blocks, spots, weights, last, dims, r, m, 0
            )
            if len(result) == 2:
                weights = result[1]
            other = send(result[0], across(0, True))
            kept = send(result[0], across(0, False))
            sent.append((kept, other))
        spots = [
            (0, (), 0, False, 0, 2 * half),
            (1, (), half, True, 0, half),
            (1, (), 0, True, half, half),
        ]
        next_own, next_peer = [], []
        for m in range(slots):
            own_term, peer_term, x_own = section(
                plan, seg_lengths, norm_gain, sent[m], spots, weights, (), dims, r, m, 1
            )
            arrived = send(peer_term, within(1))
            back = send(x_own, across(1, False))
            if r + 1 < rounds:
                new_mem = (
                    x_own[:nm].astype(F32)
                    + (own_term[:nm].astype(F32) + arrived[:nm].astype(F32))
                ).astype(BF16)
                routed = route(m, new_mem)
                next_peer.append(send(routed, across(1, True)))
                next_own.append(send(routed, across(1, False)))
            values = (x_own, own_term, arrived, back)
            if r + 1 == rounds:
                values = values[:2] + tuple(
                    pltpu.with_memory_space_constraint(v, pltpu.VMEM) for v in values[2:]
                )
            outs = finish(plan, values, outs, shapes, r, m, nm)
        mem_own, mem_peer = next_own, next_peer
    return tuple(outs)


def solution(mesh):
    specs = (
        P(None, "dp", "mp", None),
        P("dp", "mp", None),
        P(None, "dp"),
        P(),
        P("phase", None, "mp"),
        P("phase", None, "mp"),
        P("phase", None, "mp"),
        P("phase", "mp", None),
        P("phase", None),
    )
    out_specs = (P("phase", None, "dp", "mp", None), P("phase", None, "dp", "mp", None))
    step = jax.shard_map(
        per_device, mesh=mesh, in_specs=specs, out_specs=out_specs, check_vma=False
    )

    def run(segments, memory_in, *rest):
        whole = step
        return whole(segments, memory_in, *rest)

    return run
```

```python
import functools

import jax
import jax.numpy as jnp
from jax import lax
from jax.experimental import pallas as pl
from jax.experimental.pallas import tpu as pltpu
from jax.sharding import PartitionSpec as P


HEAD_SIZE = 128
EPSILON = 1e-05
TILE = 512
AXES = ("phase", "dp", "mp")
VMEM_SMALL = 14 << 20


ANY = pl.BlockSpec(memory_space=pl.ANY)
VMEM = pl.BlockSpec(memory_space=pltpu.VMEM)
SMEM = pl.BlockSpec(memory_space=pltpu.SMEM)
HBM = pl.BlockSpec(memory_space=pltpu.HBM)
BF16 = jnp.bfloat16
F32 = jnp.float32


def column(j):
    return pl.ds(pl.multiple_of(j * TILE, TILE), TILE)


def out_tile(weights, first, q_dim, j):
    per_slab = weights.shape[1] // q_dim
    return weights.at[first + j // per_slab, pl.ds(pl.multiple_of(j % per_slab * q_dim, q_dim), q_dim)]


def load_kernel(plan, w_query, weights, sem):
    copies = [
        pltpu.make_async_copy(w_query.at[:, pl.ds(n * TILE, TILE)], weights.at[n], sem.at[n])
        for n in range(w_query.shape[1] // TILE)
    ]
    for copy in copies:
        copy.start()
    for copy in copies:
        copy.wait()


def load_weights(plan, w_query, w_key, value_weight, w_out):
    width = w_query.shape[0]
    loaded = w_query.shape[1] // TILE
    tiles = (w_query.shape[1] + w_key.shape[1] + value_weight.shape[1]) // TILE
    slabs = tiles + w_out.shape[0] * w_out.shape[1] // (width * TILE)
    return pl.pallas_call(
        load_kernel,
        out_shape=pltpu.VMEM((slabs, width, TILE), BF16),
        in_specs=[SMEM, HBM],
        out_specs=VMEM,
        scratch_shapes=[pltpu.SemaphoreType.DMA((loaded,))],
        compiler_params=pltpu.CompilerParams(vmem_limit_bytes=VMEM_SMALL),
        cost_estimate=pl.CostEstimate(
            flops=0, bytes_accessed=2 * loaded * TILE * width, transcendentals=0
        ),
        name="load_weights",
    )(plan, w_query)


def section_kernel(cfg, plan, lengths, gain, *refs):
    round_index, slot, want, load, spots, q_tiles, k_tiles, half, ns = cfg
    refs = list(refs)
    blocks = [refs.pop(0) for _ in range(1 + max(s[0] for s in spots))]
    weights = refs.pop(0)
    w_key, value_weight, w_out_in = [refs.pop(0) for _ in range(3)] if load else [None] * 3
    if want:
        own_term, peer_term, x_own = [refs.pop(0) for _ in range(3)]
    else:
        term_out = refs.pop(0)
    if load:
        refs.pop(0)
    x, normed, qkv, attended = [refs.pop(0) for _ in range(4)]
    t_other = refs.pop(0) if want else None
    sem_in = refs.pop(0)
    sem_kv, sem_out = [refs.pop(0) for _ in range(2)] if load else [None] * 2
    qkv_tiles, out_tiles = q_tiles + 2 * k_tiles, weights.shape[1] // TILE
    rows, q_dim = attended.shape
    nm = half - ns

    def in_copies():
        copies = []
        for n, (ref, index, first, to_other, at, size) in enumerate(spots):
            source = blocks[ref]
            if index:
                source = source.at[index]
            target = t_other if to_other else x
            copies.append(
                pltpu.make_async_copy(
                    source.at[pl.ds(first, size)], target.at[pl.ds(at, size)], sem_in.at[n]
                )
            )
        return copies

    def out_copy(j):
        return pltpu.make_async_copy(w_out_in.at[:, column(j)], out_tile(weights, qkv_tiles, q_dim, j), sem_out.at[j])

    def kv_copies():
        return [
            pltpu.make_async_copy(
                source.at[:, pl.ds(j * TILE, TILE)],
                weights.at[q_tiles + n * k_tiles + j],
                sem_kv.at[n * k_tiles + j],
            )
            for n, source in enumerate((w_key, value_weight))
            for j in range(k_tiles)
        ]

    active = plan[0] == want
    ahead = min(4, out_tiles)

    @pl.when(active)
    def _():
        for copy in in_copies():
            copy.start()

    if load:

        @pl.when(jnp.logical_not(active))
        def _():
            copies = kv_copies() + [out_copy(j) for j in range(out_tiles)]
            for copy in copies:
                copy.start()
            for copy in copies:
                copy.wait()

    @pl.when(active)
    def _():
        for copy in in_copies():
            copy.wait()
        if load:
            for copy in kv_copies():
                copy.start()
        step = 16

        @pl.loop(0, rows // step)
        def _(b):
            at = pl.ds(pl.multiple_of(b * step, step), step)
            values = x[at, :].astype(F32)
            if want:
                rounded = (values + t_other[at, :].astype(F32)).astype(BF16)

                @pl.when(b * step < half)
                def _():
                    x_own[at, :] = rounded

                values = rounded.astype(F32)
            scale = lax.rsqrt(jnp.mean(values * values, axis=-1, keepdims=True) + EPSILON)
            normed[at, :] = (values * scale * gain[...].astype(F32)).astype(BF16)

        def project(j):
            qkv[j] = jnp.dot(normed[...], weights[j], preferred_element_type=F32).astype(BF16)

        def project_pairs(first, last):
            @pl.loop(first, last)
            def _(pair):
                for u in range(2):
                    project(pair * 2 + u)

        if load:
            project_pairs(0, 1)
            for j in range(ahead):
                out_copy(j).start()
            project_pairs(1, q_tiles // 2)
            for copy in kv_copies():
                copy.wait()
            project_pairs(q_tiles // 2, qkv_tiles // 2)
        else:
            project_pairs(0, qkv_tiles // 2)

        mp = plan[1]
        length = lengths[round_index, slot]

        def place(axis):
            at = lax.broadcasted_iota(jnp.int32, (rows, rows), axis)
            inside = lax.rem(at, half)
            owner = jnp.where(at < half, mp, 1 - mp)
            return inside < nm, inside - nm + owner * ns

        query_mem, query_seg = place(0)
        key_mem, key_seg = place(1)
        visible = key_mem | (key_seg < length) & (query_mem | (key_seg <= query_seg))
        kv_heads = k_tiles * TILE // HEAD_SIZE
        per_group = (q_tiles * TILE // HEAD_SIZE) // kv_heads
        visible = jnp.concatenate([visible] * per_group, axis=0)

        def head(base, h):
            lane = (h * HEAD_SIZE) % TILE
            return qkv[base + h * HEAD_SIZE // TILE, :, lane : lane + HEAD_SIZE]

        for c in range(kv_heads):
            heads = [c * per_group + n for n in range(per_group)]
            queries = jnp.concatenate([head(0, h) for h in heads], axis=0)
            scores = lax.dot_general(
                queries, head(q_tiles, c), (((1,), (1,)), ((), ())), preferred_element_type=F32
            ) * HEAD_SIZE ** (-0.5)
            scores = jnp.where(visible, scores, -1e30)
            exponent = jnp.exp(scores - jnp.max(scores, axis=-1, keepdims=True))
            attn = (exponent / jnp.sum(exponent, axis=-1, keepdims=True)).astype(BF16)
            result = jnp.dot(attn, head(q_tiles + k_tiles, c), preferred_element_type=F32)
            for n, h in enumerate(heads):
                attended[:, h * HEAD_SIZE : (h + 1) * HEAD_SIZE] = result[
                    n * rows : (n + 1) * rows
                ].astype(BF16)

        @pl.loop(0, out_tiles // 2)
        def _(pair):
            for u in range(2):
                j = pair * 2 + u
                if load:
                    out_copy(j).wait()

                    @pl.when(j + ahead < out_tiles)
                    def _(j=j):
                        out_copy(j + ahead).start()

                term = jnp.dot(
                    attended[...],
                    out_tile(weights, qkv_tiles, q_dim, j)[...],
                    preferred_element_type=F32,
                ).astype(BF16)
                if want:
                    own_term[:, column(j)] = term[:half]
                    peer_term[:, column(j)] = term[half:]
                else:
                    own = x[:half, column(j)].astype(F32) + term[:half].astype(F32)
                    term_out[:half, column(j)] = own.astype(BF16)
                    term_out[half:, column(j)] = term[half:]


def section(plan, lengths, gain, blocks, spots, weights, w_out, dims, round_index, slot, want):
    q_tiles, k_tiles, half, ns = dims
    load = bool(w_out)
    width = weights.shape[1]
    rows, q_dim, qkv_tiles = 2 * half, q_tiles * TILE, q_tiles + 2 * k_tiles
    weights = pltpu.with_memory_space_constraint(weights, pltpu.VMEM)
    near_blocks = (0, 1) if want else (2, 3) if round_index == 0 else (0, 2)
    blocks = [
        pltpu.with_memory_space_constraint(b, pltpu.VMEM) if n in near_blocks else b
        for n, b in enumerate(blocks)
    ]
    if want:
        out_shape = [pltpu.VMEM((half, width), BF16)] * 3
    else:
        out_shape = [pltpu.VMEM((rows, width), BF16)]
    aliases = {}
    if load:
        aliases[3 + len(blocks)] = len(out_shape)
        out_shape.append(pltpu.VMEM(weights.shape, BF16))
    scratch = [
        pltpu.VMEM((rows, width), BF16),
        pltpu.VMEM((rows, width), BF16),
        pltpu.VMEM((qkv_tiles, rows, TILE), BF16),
        pltpu.VMEM((rows, q_dim), BF16),
    ]
    if want:
        scratch.append(pltpu.VMEM((rows, width), BF16))
    scratch.append(pltpu.SemaphoreType.DMA((len(spots),)))
    if load:
        scratch.append(pltpu.SemaphoreType.DMA((2 * k_tiles,)))
        scratch.append(pltpu.SemaphoreType.DMA((width // TILE,)))
    return pl.pallas_call(
        functools.partial(
            section_kernel,
            (round_index, slot, want, load, tuple(spots), q_tiles, k_tiles, half, ns),
        ),
        out_shape=out_shape,
        in_specs=[SMEM, SMEM, VMEM] + [ANY] * len(blocks) + [VMEM] + [HBM] * len(w_out),
        out_specs=[VMEM] * len(out_shape),
        scratch_shapes=scratch,
        input_output_aliases=aliases,
        compiler_params=pltpu.CompilerParams(vmem_limit_bytes=VMEM_SMALL),
        cost_estimate=pl.CostEstimate(
            flops=2 * rows * width * (qkv_tiles * TILE + q_dim),
            bytes_accessed=2 * width * (qkv_tiles * TILE + q_dim),
            transcendentals=0,
        ),
    )(plan, lengths, gain, *blocks, weights, *w_out)


def pick_kernel(entries, count, plan, *refs):
    sources, targets, sem = refs[:count], refs[count:-1], refs[-1]

    @pl.when(plan[0] == 1)
    def _():
        for t, (target, entry) in enumerate(zip(targets, entries)):
            for n, source in enumerate(sources):

                @pl.when(plan[entry] == n)
                def _(source=source, target=target, t=t):
                    pltpu.make_async_copy(source, target, sem.at[t]).start()

        for t, target in enumerate(targets):
            pltpu.make_async_copy(sources[0], target, sem.at[t]).wait()


def pick(plan, entries, sources):
    shape = jax.ShapeDtypeStruct(sources[0].shape, sources[0].dtype)
    return pl.pallas_call(
        functools.partial(pick_kernel, tuple(entries), len(sources)),
        out_shape=[shape] * len(entries),
        in_specs=[SMEM] + [ANY] * len(sources),
        out_specs=[VMEM] * len(entries),
        scratch_shapes=[pltpu.SemaphoreType.DMA((len(entries),))],
        compiler_params=pltpu.CompilerParams(vmem_limit_bytes=4 << 20),
        name="pick",
    )(plan, *sources)


def finish_kernel(cfg, plan, x_own, own_term, arrived, back, *refs):
    round_index, slot, nm = cfg
    out_mem, out_seg, rows, term, other, sem = refs[-6:]
    half = rows.shape[0]

    def load(n, source, target):
        return pltpu.make_async_copy(source, target, sem.at[n])

    @pl.when(plan[0] == 0)
    def _():
        copy = load(0, back, rows)
        copy.start()
        copy.wait()

    @pl.when(plan[0] != 0)
    def _():
        copies = [load(0, x_own, rows), load(1, own_term, term), load(2, arrived, other)]
        for copy in copies:
            copy.start()
        for copy in copies:
            copy.wait()
        step = 16

        @pl.loop(0, half // step)
        def _(b):
            at = pl.ds(pl.multiple_of(b * step, step), step)
            added = term[at, :].astype(F32) + other[at, :].astype(F32)
            rows[at, :] = (rows[at, :].astype(F32) + added).astype(BF16)

    copies = [
        load(0, rows.at[pl.ds(0, nm)], out_mem.at[0, round_index, slot]),
        load(1, rows.at[pl.ds(nm, half - nm)], out_seg.at[0, round_index, slot]),
    ]
    for copy in copies:
        copy.start()
    for copy in copies:
        copy.wait()


def finish(plan, values, outs, shapes, round_index, slot, nm):
    half, width = values[0].shape
    return pl.pallas_call(
        functools.partial(finish_kernel, (round_index, slot, nm)),
        out_shape=[jax.ShapeDtypeStruct(shape, BF16) for shape in shapes],
        in_specs=[SMEM] + [ANY] * (4 + len(outs)),
        out_specs=[HBM] * 2,
        scratch_shapes=[pltpu.VMEM((half, width), BF16)] * 3 + [pltpu.SemaphoreType.DMA((3,))],
        input_output_aliases={5 + n: n for n in range(len(outs))},
        compiler_params=pltpu.CompilerParams(vmem_limit_bytes=4 << 20),
    )(plan, *values, *outs)


def per_device(
    segments, memory_in, seg_lengths, routes, w_query, w_key, value_weight, w_out, norm_gain
):
    rounds, slots = segments.shape[0], segments.shape[1]
    nm, ns = memory_in.shape[1], segments.shape[2]
    half = nm + ns
    groups = lax.axis_size("dp")
    phase, group, mp = (lax.axis_index(a) for a in AXES)
    inner = 2 if groups % 2 == 0 else 1
    outer = groups // inner

    def flat(p, g, i):
        return (p * groups + g) * 2 + i

    def send(value, pairs_of):
        pairs = [pair for g in range(groups) for i in range(2) for pair in pairs_of(g, i)]
        return lax.ppermute(value, AXES, pairs)

    def within(p):
        return lambda g, i: [(flat(p, g, i), flat(p, g, 1 - i))]

    def across(p, flip):
        return lambda g, i: [(flat(p, g, i), flat(1 - p, g, 1 - i if flip else i))]

    def hop(place, step):
        return place ^ step if outer & (outer - 1) == 0 else (place + step) % outer

    def along(step_outer, step_inner):
        def pairs(g, i):
            o, n = divmod(g, inner)
            target = hop(o, step_outer) * inner + (n + step_inner) % inner
            return [(flat(1, g, i), flat(1, target, i))]

        return pairs

    ids = jnp.arange(groups, dtype=jnp.int32)
    mine_o, mine_n = group // inner, group % inner
    targets = mine_o * inner + (mine_n + jnp.arange(inner, dtype=jnp.int32)) % inner
    hit = routes[:, None, :] == targets[None, :, None]
    source = jnp.sum(jnp.where(hit, ids[None, None, :], 0), axis=-1)
    source_o = source // inner
    if outer & (outer - 1) == 0:
        hops = (mine_o ^ source_o) & (outer - 1)
    else:
        hops = (mine_o - source_o + outer) % outer
    side = (mine_n - source[:, :1] % inner + inner) % inner
    entries = 1 + inner
    plan = jnp.concatenate(
        [
            jnp.stack([phase, mp]).astype(jnp.int32),
            jnp.concatenate([hops, side], axis=1).reshape(slots * entries),
        ]
    )

    def route(m, rows):
        base = 2 + m * entries
        held = {0: rows}
        if outer & (outer - 1) == 0:
            bit = outer // 2
            while bit:
                for k in sorted(held, reverse=True):
                    if k ^ bit not in held:
                        held[k ^ bit] = send(held[k], along(bit, 0))
                bit //= 2
        else:
            for k in range(1, outer):
                held[k] = send(rows, along(k, 0))
        held = [held[k] for k in range(outer)]
        picked = pick(plan, [base + k for k in range(inner)], held)
        if inner == 1:
            return picked[0]
        arrived = [send(picked[k], along(0, k)) for k in range(1, inner)]
        return pick(plan, [base + inner], [picked[0]] + arrived)[0]

    weights = load_weights(plan, w_query[0], w_key[0], value_weight[0], w_out[0])
    dims = (w_query.shape[2] // TILE, w_key.shape[2] // TILE, half, ns)
    first_mem = send(memory_in, within(0))
    first_seg = send(segments[:1], within(0))
    later_peer = None
    if rounds > 1:
        later_peer = send(segments[1:], within(1))
        later_peer = send(later_peer, across(1, False))
    mem_own = mem_peer = None
    shapes = [(1, rounds, slots, n) + memory_in.shape[2:] for n in (nm, ns)]
    outs = []
    for r in range(rounds):
        sent = []
        for m in range(slots):
            if r == 0:
                blocks = [memory_in, segments, first_mem, first_seg]
                spots = [
                    (0, (m,), 0, False, 0, nm),
                    (1, (0, m), 0, False, nm, ns),
                    (2, (m,), 0, False, half, nm),
                    (3, (0, m), 0, False, half + nm, ns),
                ]
            else:
                blocks = [mem_own[m], segments, mem_peer[m], later_peer]
                spots = [
                    (0, (), 0, False, 0, nm),
                    (1, (r, m), 0, False, nm, ns),
                    (2, (), 0, False, half, nm),
                    (3, (r - 1, m), 0, False, half + nm, ns),
                ]
            last = (w_key[0], value_weight[0], w_out[0]) if r == 0 and m == 0 else ()
            result = section(
                plan, seg_lengths, norm_gain, blocks, spots, weights, last, dims, r, m, 0
            )
            if len(result) == 2:
                weights = result[1]
            other = send(result[0], across(0, True))
            kept = send(result[0], across(0, False))
            sent.append((kept, other))
        spots = [
            (0, (), 0, False, 0, 2 * half),
            (1, (), half, True, 0, half),
            (1, (), 0, True, half, half),
        ]
        next_own, next_peer = [], []
        for m in range(slots):
            own_term, peer_term, x_own = section(
                plan, seg_lengths, norm_gain, sent[m], spots, weights, (), dims, r, m, 1
            )
            arrived = send(peer_term, within(1))
            back = send(x_own, across(1, False))
            if r + 1 < rounds:
                new_mem = (
                    x_own[:nm].astype(F32)
                    + (own_term[:nm].astype(F32) + arrived[:nm].astype(F32))
                ).astype(BF16)
                routed = route(m, new_mem)
                next_peer.append(send(routed, across(1, True)))
                next_own.append(send(routed, across(1, False)))
            values = (x_own, own_term, arrived, back)
            if r + 1 == rounds:
                values = values[:2] + tuple(
                    pltpu.with_memory_space_constraint(v, pltpu.VMEM) for v in values[2:]
                )
            outs = finish(plan, values, outs, shapes, r, m, nm)
        mem_own, mem_peer = next_own, next_peer
    return tuple(outs)


def solution(mesh):
    specs = (
        P(None, "dp", "mp", None),
        P("dp", "mp", None),
        P(None, "dp"),
        P(),
        P("phase", None, "mp"),
        P("phase", None, "mp"),
        P("phase", None, "mp"),
        P("phase", "mp", None),
        P("phase", None),
    )
    out_specs = (P("phase", None, "dp", "mp", None), P("phase", None, "dp", "mp", None))
    step = jax.shard_map(
        per_device, mesh=mesh, in_specs=specs, out_specs=out_specs, check_vma=False
    )

    def run(segments, memory_in, *rest):
        whole = step
        return whole(segments, memory_in, *rest)

    return run
```
